32 devices in a mesh: dp: 8 (over z, core), graph: 4 (over y, x).
Axes of the slice: x: 2, y: 2, z: 4, core: 2. Of those that a mesh axis runs over, the one named last changes fastest.
Arguments:
- edge_feats: bfloat16 [32768, 512], P(('dp', 'graph')), may hold values from -6 to 6
- cotangent: bfloat16 [32768, 512], P(('dp', 'graph')), may hold values from -6 to 6
- angle_basis: bfloat16 [16, 262144], P(None, ('dp', 'graph')), may hold values from -6 to 6
- source_edge: int32 [262144], P(('dp', 'graph')), may hold values from 0 to 4095
- target_edge: int32 [262144], P(('dp', 'graph')), may hold values from 0 to 1023
- pair_weight: bfloat16 [512, 512], P('dp'), may hold values from -0.25 to 0.25
- down_weight: bfloat16 [512, 64], P('dp'), may hold values from -0.25 to 0.25
- basis_weight: bfloat16 [16, 64], P('dp'), may hold values from -1.5 to 1.5
- up_weight: bfloat16 [64, 512], P('dp'), may hold values from -0.75 to 0.75
- res_first: bfloat16 [512, 512], P('dp'), may hold values from -0.25 to 0.25
- res_second: bfloat16 [512, 512], P('dp'), may hold values from -0.25 to 0.25
Outputs:
- edge_grad: bfloat16 [32768, 512], P(('dp', 'graph'))
- pair_grad: float32 [512, 512], P('dp')
- down_grad: float32 [512, 64], P('dp')
- basis_grad: float32 [16, 64], P('dp')
- up_grad: float32 [64, 512], P('dp')
- first_grad: float32 [512, 512], P('dp')
- second_grad: float32 [512, 512], P('dp')
The draws below stay inside these ranges and needn't reach their ends.
Inputs may be any that keep to these rules, and one draw needn't show every extreme that they name: source_edge[t] may name any edge of the 4 devices of the triplet's group. target_edge[t] names an edge of the triplet's own device.
All inputs are finite; a program needn't handle non-finite values.
Results may differ from the reference program's by a relative error of at most 0.013.
Values may be sent and summed in bfloat16 or wider, within the bound.
A program may use at most 64 MiB of HBM per device.

```python
import math
import jax
import jax.numpy as jnp
from jax import lax

D = 512
DT = 64
NCBF = 16
E_DEV = 1024
T_DEV = 8192
E_GRP = 4096
T_GRP = 32768
EDGES = 32768
TRIPS = 262144
N_DP = 8


def set_ends(entries, key, smallest, high):
    shape = entries.shape
    index_at = [jax.random.randint(jax.random.fold_in(key, axis), (), 0, shape[axis]) for axis in range(len(shape))]
    entries = entries.at[tuple(index_at)].set(smallest)
    longest = shape.index(max(shape))
    index_at[longest] = (index_at[longest] + 1) % shape[longest]
    return entries.at[tuple(index_at)].set(high)


def spiked(drawn, stream_key, source, target, blocks, factor):
    owner, partner = [(jnp.arange(drawn.shape[dim]) // (drawn.shape[dim] // blocks)).reshape([-1 if axis == dim else 1 for axis in range(drawn.ndim)]) for dim in (source, target)]
    chosen = jax.random.permutation(stream_key, blocks)[partner]
    strong = (owner == chosen) | (owner == (partner + blocks // 2) % blocks)
    return jnp.where(strong, factor * drawn, drawn)


def block_scale(rng, extent, shards, least, high):
    def one(dim, blocks):
        draws = jax.random.uniform(jax.random.fold_in(jax.random.fold_in(rng, 6), dim), (blocks,), jnp.float32, least / len(shards), high / len(shards))
        return jnp.repeat(jnp.exp(draws), extent[dim] // blocks).reshape((-1,) + (1,) * (len(extent) - dim - 1))

    loudness = one(*shards[0])
    for cut in shards[1:]:
        loudness = loudness * one(*cut)
    return loudness


def noise(stream_key, shape, deviation, most, shards=(), held_as=jnp.bfloat16):
    array = jax.random.normal(stream_key, shape, jnp.float32) * deviation
    if len(shards) > 0:
        array = block_scale(stream_key, shape, shards, -0.22, 0.18) * array
    return jnp.clip(array, min=-most, max=most).astype(held_as)


def noise_with(rng, dims, deviation, limit, shards, heavy, kind=jnp.bfloat16):
    result = deviation * jax.random.normal(rng, dims, jnp.float32)
    if shards:
        result = result * block_scale(rng, dims, shards, -0.22, 0.18)
    return jnp.clip(spiked(result, jax.random.fold_in(rng, 3), *heavy), -limit, limit).astype(kind)


def setup_inputs(seed: int = 0) -> dict:
    streams_of = jax.random.split(jax.random.key(seed), 12)
    edge_feats = noise_with(streams_of[0], (EDGES, D), 1.0, 6.0, ((0, 32),), (0, 1, 32, 2.75))
    cotangent = noise(streams_of[1], (EDGES, D), 1.0, 6.0, ((0, 32),))
    angle_basis = noise(streams_of[2], (NCBF, TRIPS), 1.0, 6.0, ((1, 32),))
    source_edge = set_ends(jax.random.randint(streams_of[3], (TRIPS,), 0, E_GRP), jax.random.fold_in(streams_of[3], 1), 0, E_GRP - 1).astype(jnp.int32)
    target_edge = set_ends(jax.random.randint(streams_of[4], (TRIPS,), 0, E_DEV), jax.random.fold_in(streams_of[4], 1), 0, E_DEV - 1).astype(jnp.int32)
    pair_weight = noise(streams_of[5], (D, D), D ** -0.5, 0.25, ((0, 8),))
    down_weight = noise(streams_of[6], (D, DT), D ** -0.5, 0.25, ((0, 8),))
    basis_weight = noise(streams_of[7], (NCBF, DT), NCBF ** -0.5, 1.5, ((0, 8),))
    up_weight = noise(streams_of[8], (DT, D), DT ** -0.5, 0.75, ((0, 8),))
    res_first = noise(streams_of[9], (D, D), D ** -0.5, 0.25, ((0, 8),))
    res_second = noise(streams_of[10], (D, D), D ** -0.5, 0.25, ((0, 8),))
    return {"edge_feats": edge_feats, "cotangent": cotangent, "angle_basis": angle_basis, "source_edge": source_edge, "target_edge": target_edge, "pair_weight": pair_weight, "down_weight": down_weight, "basis_weight": basis_weight, "up_weight": up_weight, "res_first": res_first, "res_second": res_second}


def silu_slope(value):
    sig = jax.nn.sigmoid(value)
    return sig * (1.0 + value * (1.0 - sig))

def group_pass(feats, cotan, basis, source, target, pair_weight, down_weight, basis_weight, up_weight, res_first, res_second):
    f32 = jnp.float32
    bf16 = jnp.bfloat16
    scale = math.sqrt(0.5)
    offset = jnp.arange(T_GRP, dtype=jnp.int32) // T_DEV * E_DEV
    outgoing = target + offset
    z_one = jnp.dot(feats, pair_weight, preferred_element_type=f32)
    hidden = jax.nn.silu(z_one).astype(bf16)
    down_t = jnp.einsum('ed,dk->ke', hidden.astype(f32), down_weight.astype(f32)).astype(bf16)
    coeff = jnp.einsum('nk,nt->kt', basis_weight.astype(f32), basis.astype(f32))
    down_in = down_t[:, source].astype(f32)
    agg_t = jnp.zeros((DT, E_GRP), f32).at[:, outgoing].add(down_in * coeff).astype(bf16)
    z_two = jnp.einsum('ke,kd->ed', agg_t.astype(f32), up_weight.astype(f32))
    mixed = jax.nn.silu(z_two).astype(bf16)
    z_three = jnp.dot(mixed, res_first, preferred_element_type=f32)
    inner = jax.nn.silu(z_three).astype(bf16)
    z_four = jnp.dot(inner, res_second, preferred_element_type=f32)
    dz_four = (scale * cotan.astype(f32) * silu_slope(z_four)).astype(bf16)
    second_grad = jnp.dot(inner.T, dz_four, preferred_element_type=f32)
    dz_three = (jnp.dot(dz_four, res_second.T, preferred_element_type=f32) * silu_slope(z_three)).astype(bf16)
    first_grad = jnp.dot(mixed.T, dz_three, preferred_element_type=f32)
    dmixed = scale * cotan.astype(f32) + jnp.dot(dz_three, res_first.T, preferred_element_type=f32)
    dz_two = (dmixed * silu_slope(z_two)).astype(bf16)
    up_grad = jnp.einsum('ke,ed->kd', agg_t.astype(f32), dz_two.astype(f32))
    dagg_t = jnp.einsum('kd,ed->ke', up_weight.astype(f32), dz_two.astype(f32))
    dagg_out = dagg_t[:, outgoing]
    dcoeff = (dagg_out * down_in).astype(bf16)
    basis_grad = jnp.einsum('nt,kt->nk', basis.astype(f32), dcoeff.astype(f32))
    ddown_t = jnp.zeros((DT, E_GRP), f32).at[:, source].add(dagg_out * coeff).astype(bf16)
    down_grad = jnp.einsum('ed,ke->dk', hidden.astype(f32), ddown_t.astype(f32))
    dz_one = (jnp.einsum('ke,dk->ed', ddown_t.astype(f32), down_weight.astype(f32)) * silu_slope(z_one)).astype(bf16)
    pair_grad = jnp.dot(feats.T, dz_one, preferred_element_type=f32)
    edge_grad = jnp.dot(dz_one, pair_weight.T, preferred_element_type=f32).astype(bf16)
    return (edge_grad, (pair_grad, down_grad, basis_grad, up_grad, first_grad, second_grad))

def reference(edge_feats, cotangent, angle_basis, source_edge, target_edge, pair_weight, down_weight, basis_weight, up_weight, res_first, res_second):
    feats = edge_feats.reshape(N_DP, E_GRP, D)
    cotans = cotangent.reshape(N_DP, E_GRP, D)
    bases = jnp.transpose(angle_basis.reshape(NCBF, N_DP, T_GRP), (1, 0, 2))
    sources = source_edge.reshape(N_DP, T_GRP)
    targets = target_edge.reshape(N_DP, T_GRP)
    weights = (pair_weight, down_weight, basis_weight, up_weight, res_first, res_second)
    start = tuple((jnp.zeros(w.shape, jnp.float32) for w in weights))

    def step(carry, items):
        grads, parts = group_pass(items[0], items[1], items[2], items[3], items[4], *weights)
        summed = tuple((c + p for c, p in zip(carry, parts)))
        return (summed, grads)
    totals, grads = lax.scan(step, start, (feats, cotans, bases, sources, targets))
    edge_grad = grads.reshape(EDGES, D)
    return (edge_grad, totals[0], totals[1], totals[2], totals[3], totals[4], totals[5])
```

```python
import functools
import math

import jax
import jax.numpy as jnp
from jax import lax
from jax.experimental import pallas as pl
from jax.experimental.pallas import tpu as pltpu
from jax.sharding import PartitionSpec as P

MESH = pl.DeviceIdType.MESH
F32 = jnp.float32
BF16 = jnp.bfloat16
VM = pl.BlockSpec(memory_space=pltpu.VMEM)
SUB = 256
TILE = 1024


def remote(src, dst, send, recv, target):
    return pltpu.make_async_remote_copy(
        src_ref=src,
        dst_ref=dst,
        send_sem=send,
        recv_sem=recv,
        device_id=target,
        device_id_type=MESH,
    )


def silu_slope(value):
    sig = jax.nn.sigmoid(value)
    return sig * (1.0 + value * (1.0 - sig))


def gather_kernel(n, count, *refs):
    ins, outs = refs[:count], refs[count : 2 * count]
    send, recv = refs[2 * count :]
    half = n // 2
    dp = lax.axis_index("dp")
    pos = dp // 2
    core = dp % 2
    partner = dp + 1 - 2 * core
    has_up = pos < half - 1
    has_down = pos > 0
    barrier = pltpu.get_barrier_semaphore()

    @pl.when(has_up)
    def _():
        pl.semaphore_signal(barrier, inc=1, device_id={"dp": dp + 2}, device_id_type=MESH)

    @pl.when(has_down)
    def _():
        pl.semaphore_signal(barrier, inc=1, device_id={"dp": dp - 2}, device_id_type=MESH)

    pl.semaphore_signal(barrier, inc=1, device_id={"dp": partner}, device_id_type=MESH)

    pl.semaphore_wait(barrier, 1 + has_up.astype(jnp.int32) + has_down.astype(jnp.int32))

    def copy(w, src, shard, way, target):
        return remote(
            src, outs[w].at[shard], send.at[shard, way, w], recv.at[shard, w], {"dp": target}
        )

    for w in range(count):

        @pl.when(has_up)
        def _():
            copy(w, ins[w], dp, 0, dp + 2).start()

        @pl.when(has_down)
        def _():
            copy(w, ins[w], dp, 1, dp - 2).start()

        copy(w, ins[w], dp, 2, partner).start()
    for w in range(count):
        outs[w][dp] = ins[w][...]
    for k in range(1, half):
        for w in range(count):

            @pl.when(pos >= k)
            def _():
                shard = dp - 2 * k
                block = outs[w].at[shard]
                copy(w, block, shard, 2, partner).wait_recv()

                @pl.when(has_up)
                def _():
                    copy(w, block, shard, 0, dp + 2).start()

                copy(w, block, shard, 2, partner).start()

            @pl.when(pos + k < half)
            def _():
                shard = dp + 2 * k
                block = outs[w].at[shard]
                copy(w, block, shard, 2, partner).wait_recv()

                @pl.when(has_down)
                def _():
                    copy(w, block, shard, 1, dp - 2).start()

                copy(w, block, shard, 2, partner).start()

    for w in range(count):
        for q in range(half):
            shard = 2 * q + 1 - core
            copy(w, outs[w].at[shard], shard, 2, partner).wait_recv()
            mine = 2 * q + core
            copy(w, outs[w].at[mine], mine, 2, partner).wait_send()

            @pl.when(jnp.logical_and(pos >= q, has_up))
            def _():
                copy(w, outs[w].at[mine], mine, 0, dp + 2).wait_send()

            @pl.when(jnp.logical_and(pos <= q, has_down))
            def _():
                copy(w, outs[w].at[mine], mine, 1, dp - 2).wait_send()


def gather_weights(n, weights):
    count = len(weights)
    return pl.pallas_call(
        functools.partial(gather_kernel, n, count),
        out_shape=[jax.ShapeDtypeStruct((n,) + w.shape, w.dtype) for w in weights],
        in_specs=[VM] * count,
        out_specs=[VM] * count,
        scratch_shapes=[
            pltpu.SemaphoreType.DMA((n, 3, count)),
            pltpu.SemaphoreType.DMA((n, count)),
        ],
        compiler_params=pltpu.CompilerParams(collective_id=0, has_side_effects=True),
        name="gather_weights",
    )(*weights)


def greet_graph(groups, me):
    barrier = pltpu.get_barrier_semaphore()
    for k in range(1, groups):
        pl.semaphore_signal(
            barrier, inc=1, device_id={"graph": (me + k) % groups}, device_id_type=MESH
        )
    pl.semaphore_wait(barrier, groups - 1)


def spread_kernel(groups, in_ref, out_ref, send, recv):
    me = lax.axis_index("graph")
    greet_graph(groups, me)
    copies = []
    for k in range(1, groups):
        cp = remote(
            in_ref, out_ref.at[me], send.at[k], recv.at[k], {"graph": (me + k) % groups}
        )
        cp.start()
        copies.append(cp)
    out_ref[me] = in_ref[...]
    for cp in copies:
        cp.wait()


def spread_down(groups, block):
    return pl.pallas_call(
        functools.partial(spread_kernel, groups),
        out_shape=jax.ShapeDtypeStruct((groups,) + block.shape, block.dtype),
        in_specs=[VM],
        out_specs=VM,
        scratch_shapes=[pltpu.SemaphoreType.DMA((groups,))] * 2,
        compiler_params=pltpu.CompilerParams(collective_id=1, has_side_effects=True),
        name="spread_down",
    )(block)


def collect_kernel(groups, in_ref, out_ref, landed, send, recv):
    me = lax.axis_index("graph")
    greet_graph(groups, me)
    copies = []
    for k in range(1, groups):
        peer = (me + k) % groups
        cp = remote(in_ref.at[peer], landed.at[k], send.at[k], recv.at[k], {"graph": peer})
        cp.start()
        copies.append(cp)
    for cp in copies:
        cp.wait()
    total = in_ref[me].astype(F32)
    for k in range(1, groups):
        total = total + landed[k].astype(F32)
    out_ref[...] = total.astype(out_ref.dtype)


def collect_down(groups, partial):
    shape = partial.shape[1:]
    return pl.pallas_call(
        functools.partial(collect_kernel, groups),
        out_shape=jax.ShapeDtypeStruct(shape, BF16),
        in_specs=[VM],
        out_specs=VM,
        scratch_shapes=[pltpu.VMEM(partial.shape, partial.dtype)]
        + [pltpu.SemaphoreType.DMA((groups,))] * 2,
        compiler_params=pltpu.CompilerParams(collective_id=2, has_side_effects=True),
        name="collect_down",
    )(partial)


def total_kernel(n, groups, kinds, *refs):
    count = len(kinds)
    ins, outs = refs[:count], refs[count : 2 * count]
    pos_in = 2 * count
    scratch = []
    for large in kinds:
        size = 7 if large else 5
        scratch.append(refs[pos_in : pos_in + size])
        pos_in += size
    a_send, a_recv, b_send, b_recv, c_send, c_recv, d_send, d_recv = refs[pos_in:]
    half = n // 2
    dp = lax.axis_index("dp")
    me = lax.axis_index("graph")
    pos = dp // 2
    core = dp % 2
    partner = dp + 1 - 2 * core
    barrier = pltpu.get_barrier_semaphore()
    pl.semaphore_signal(barrier, inc=1, device_id={"dp": partner}, device_id_type=MESH)
    for k in range(1, groups):
        pl.semaphore_signal(
            barrier, inc=1, device_id={"graph": (me + k) % groups}, device_id_type=MESH
        )
    for k in range(1, half):
        pl.semaphore_signal(
            barrier,
            inc=1,
            device_id={"dp": (pos + k) % half * 2 + core},
            device_id_type=MESH,
        )
    pl.semaphore_wait(barrier, groups + half - 1)

    sent = []

    def send_all(copies):
        for cp in copies:
            cp.start()
        sent.extend(copies)
        return copies

    first = []
    for w in range(count):
        first.append(
            send_all(
                [
                    remote(
                        ins[w].at[2 * q + 1 - core],
                        scratch[w][0].at[q],
                        a_send.at[w, q],
                        a_recv.at[w, q],
                        {"dp": partner},
                    )
                    for q in range(half)
                ]
            )
        )
    second = []
    for w, large in enumerate(kinds):
        got, summed = scratch[w][0], scratch[w][1]
        for q in range(half):
            first[w][q].wait_recv()
            value = ins[w][2 * q + core].astype(F32) + got[q].astype(F32)
            if large:
                summed[:, q] = value.astype(summed.dtype)
            else:
                summed[q] = value.astype(summed.dtype)
        if large:
            second.append(
                send_all(
                    [
                        remote(
                            summed.at[(me + k) % groups],
                            scratch[w][5].at[k],
                            b_send.at[w, k],
                            b_recv.at[w, k],
                            {"graph": (me + k) % groups},
                        )
                        for k in range(1, groups)
                    ]
                )
            )
        else:
            second.append([])
    third = []
    for w, large in enumerate(kinds):
        if large:
            for cp in second[w]:
                cp.wait_recv()
            value = scratch[w][1][me].astype(F32)
            for k in range(1, groups):
                value = value + scratch[w][5][k].astype(F32)
            part = scratch[w][6]
            part[...] = value.astype(part.dtype)
        else:
            part = scratch[w][1]
        third.append(
            send_all(
                [
                    remote(
                        part.at[(pos + k) % half],
                        scratch[w][2].at[k],
                        c_send.at[w, k],
                        c_recv.at[w, k],
                        {"dp": (pos + k) % half * 2 + core},
                    )
                    for k in range(1, half)
                ]
            )
        )
    fourth = []
    for w, large in enumerate(kinds):
        part = scratch[w][6] if large else scratch[w][1]
        for cp in third[w]:
            cp.wait_recv()
        value = part[pos].astype(F32)
        for k in range(1, half):
            value = value + scratch[w][2][k].astype(F32)
        done = scratch[w][3]
        done[...] = value.astype(done.dtype)
        fourth.append(
            send_all(
                [
                    remote(
                        done,
                        scratch[w][4].at[me],
                        d_send.at[w, k],
                        d_recv.at[w, k],
                        {"graph": (me + k) % groups},
                    )
                    for k in range(1, groups)
                ]
            )
        )
        scratch[w][4][me] = value.astype(done.dtype)
    for w, large in enumerate(kinds):
        for cp in fourth[w]:
            cp.wait_recv()
        landed = scratch[w][4]
        if large:
            outs[w][...] = landed[...].astype(F32)
        else:
            value = landed[0].astype(F32)
            for g in range(1, groups):
                value = value + landed[g].astype(F32)
            outs[w][...] = value
    for cp in sent:
        cp.wait_send()


def total_grads(n, groups, grads, kinds):
    half = n // 2
    shapes, scratch = [], []
    for item, large in zip(grads, kinds):
        tail = item.shape[2:] if large else item.shape[1:]
        kind = item.dtype
        shapes.append(jax.ShapeDtypeStruct(((groups,) if large else ()) + tail, F32))
        scratch.append(pltpu.VMEM((half,) + item.shape[1:], kind))
        scratch.append(
            pltpu.VMEM(((groups, half) + tail) if large else ((half,) + tail), kind)
        )
        scratch.append(pltpu.VMEM((half,) + tail, kind))
        scratch.append(pltpu.VMEM(tail, kind))
        scratch.append(pltpu.VMEM((groups,) + tail, kind))
        if large:
            scratch.append(pltpu.VMEM((groups, half) + tail, kind))
            scratch.append(pltpu.VMEM((half,) + tail, kind))
    count = len(grads)
    sems = []
    for width in (half, groups, half, groups):
        sems += [pltpu.SemaphoreType.DMA((count, width))] * 2
    return pl.pallas_call(
        functools.partial(total_kernel, n, groups, kinds),
        out_shape=shapes,
        in_specs=[VM] * count,
        out_specs=[VM] * count,
        scratch_shapes=scratch + sems,
        compiler_params=pltpu.CompilerParams(collective_id=3, has_side_effects=True),
        name="total_grads",
    )(*grads)


def one_hot(size, row):
    spots = lax.broadcasted_iota(jnp.int32, (size, row.shape[1]), 0)
    return jnp.where(spots == row, 1.0, 0.0).astype(BF16)


def pick(stack, owner, groups, width):
    value = jnp.where(owner == 0, stack[:width], 0.0)
    for g in range(1, groups):
        value = value + jnp.where(owner == g, stack[g * width : (g + 1) * width], 0.0)
    return value


def place(value, owner, groups):
    return jnp.concatenate(
        [jnp.where(owner == g, value, 0.0).astype(BF16) for g in range(groups)], axis=0
    )


def dot(a, b, dims):
    return lax.dot_general(a, b, (dims, ((), ())), preferred_element_type=F32)


NN = ((1,), (0,))
NT = ((1,), (1,))
TN = ((0,), (0,))


def forward_kernel(
    groups, edges, width, src_ref, tgt_ref, basis_ref, wb_ref, table_ref, agg_ref, din_ref, acc
):
    step = pl.program_id(0)
    subs = edges // SUB

    @pl.when(step == 0)
    def _():
        acc[...] = jnp.zeros_like(acc)

    src = src_ref[...]
    tgt = tgt_ref[...]
    owner = src // edges
    stack = dot(table_ref[...], one_hot(edges, src - owner * edges), NN)
    down_in = pick(stack, owner, groups, width)
    din_ref[...] = down_in.astype(BF16)
    coeff = dot(wb_ref[...], basis_ref[...], TN)
    high = tgt // SUB
    acc[...] += dot(place(down_in * coeff, high, subs), one_hot(SUB, tgt - high * SUB), NT)

    @pl.when(step == pl.num_programs(0) - 1)
    def _():
        for h in range(subs):
            agg_ref[:, h * SUB : (h + 1) * SUB] = acc[h * width : (h + 1) * width, :].astype(BF16)


def forward_triplets(groups, edges, src, tgt, basis, w_basis, table):
    trips = src.shape[1]
    width = w_basis.shape[1]
    tile = min(TILE, trips)
    row = pl.BlockSpec((1, tile), lambda i: (0, i))
    return pl.pallas_call(
        functools.partial(forward_kernel, groups, edges, width),
        grid=(trips // tile,),
        out_shape=[
            jax.ShapeDtypeStruct((width, edges), BF16),
            jax.ShapeDtypeStruct((width, trips), BF16),
        ],
        in_specs=[
            row,
            row,
            pl.BlockSpec((basis.shape[0], tile), lambda i: (0, i)),
            pl.BlockSpec(w_basis.shape, lambda i: (0, 0)),
            pl.BlockSpec(table.shape, lambda i: (0, 0)),
        ],
        out_specs=[
            pl.BlockSpec((width, edges), lambda i: (0, 0)),
            pl.BlockSpec((width, tile), lambda i: (0, i)),
        ],
        scratch_shapes=[pltpu.VMEM((edges // SUB * width, SUB), F32)],
        name="forward_triplets",
    )(src, tgt, basis, w_basis, table)


def backward_kernel(
    groups,
    edges,
    width,
    src_ref,
    tgt_ref,
    basis_ref,
    wb_ref,
    din_ref,
    dagg_ref,
    part_ref,
    bg_ref,
    acc,
    stack_ref,
):
    step = pl.program_id(0)
    subs = edges // SUB

    @pl.when(step == 0)
    def _():
        acc[...] = jnp.zeros_like(acc)
        bg_ref[...] = jnp.zeros_like(bg_ref)
        for h in range(subs):
            stack_ref[h * width : (h + 1) * width, :] = dagg_ref[:, h * SUB : (h + 1) * SUB]

    src = src_ref[...]
    tgt = tgt_ref[...]
    owner = src // edges
    high = tgt // SUB
    dagg_out = pick(
        dot(stack_ref[...], one_hot(SUB, tgt - high * SUB), NN), high, subs, width
    )
    dcoeff = (dagg_out * din_ref[...].astype(F32)).astype(BF16)
    bg_ref[...] += dot(basis_ref[...], dcoeff, NT)
    coeff = dot(wb_ref[...], basis_ref[...], TN)
    acc[...] += dot(
        place(dagg_out * coeff, owner, groups), one_hot(edges, src - owner * edges), NT
    )

    @pl.when(step == pl.num_programs(0) - 1)
    def _():
        part_ref[...] = acc[...].astype(BF16)


def backward_triplets(groups, edges, src, tgt, basis, w_basis, down_in, dagg):
    trips = src.shape[1]
    width = w_basis.shape[1]
    tile = min(TILE, trips)
    row = pl.BlockSpec((1, tile), lambda i: (0, i))
    return pl.pallas_call(
        functools.partial(backward_kernel, groups, edges, width),
        grid=(trips // tile,),
        out_shape=[
            jax.ShapeDtypeStruct((groups * width, edges), BF16),
            jax.ShapeDtypeStruct(w_basis.shape, F32),
        ],
        in_specs=[
            row,
            row,
            pl.BlockSpec((basis.shape[0], tile), lambda i: (0, i)),
            pl.BlockSpec(w_basis.shape, lambda i: (0, 0)),
            pl.BlockSpec((width, tile), lambda i: (0, i)),
            pl.BlockSpec(dagg.shape, lambda i: (0, 0)),
        ],
        out_specs=[
            pl.BlockSpec((groups * width, edges), lambda i: (0, 0)),
            pl.BlockSpec(w_basis.shape, lambda i: (0, 0)),
        ],
        scratch_shapes=[
            pltpu.VMEM((groups * width, edges), F32),
            pltpu.VMEM((edges // SUB * width, SUB), BF16),
        ],
        name="backward_triplets",
    )(src, tgt, basis, w_basis, down_in, dagg)


def on_device(
    edge_feats,
    cotangent,
    angle_basis,
    source_edge,
    target_edge,
    pair_weight,
    down_weight,
    basis_weight,
    up_weight,
    res_first,
    res_second,
):
    scale = math.sqrt(0.5)
    n = lax.axis_size("dp")
    groups = lax.axis_size("graph")
    w_pair, w_down, w_basis, w_up, w_first, w_second = [
        item.reshape(-1, item.shape[2])
        for item in gather_weights(
            n, (pair_weight, down_weight, basis_weight, up_weight, res_first, res_second)
        )
    ]
    edges = edge_feats.shape[0]
    width = w_down.shape[1]
    src = source_edge.reshape(1, -1)
    tgt = target_edge.reshape(1, -1)
    z_one = jnp.dot(edge_feats, w_pair, preferred_element_type=F32)
    hidden = jax.nn.silu(z_one).astype(BF16)
    down_t = jnp.einsum("ed,dk->ke", hidden, w_down, preferred_element_type=F32).astype(BF16)
    table = spread_down(groups, down_t).reshape(groups * width, edges)
    agg_t, down_in = forward_triplets(groups, edges, src, tgt, angle_basis, w_basis, table)
    z_two = jnp.einsum("ke,kd->ed", agg_t, w_up, preferred_element_type=F32)
    mixed = jax.nn.silu(z_two).astype(BF16)
    z_three = jnp.dot(mixed, w_first, preferred_element_type=F32)
    inner = jax.nn.silu(z_three).astype(BF16)
    z_four = jnp.dot(inner, w_second, preferred_element_type=F32)
    dz_four = (scale * cotangent.astype(F32) * silu_slope(z_four)).astype(BF16)
    dz_three = (
        jnp.einsum("ed,fd->ef", dz_four, w_second, preferred_element_type=F32) * silu_slope(z_three)
    ).astype(BF16)
    dmixed = scale * cotangent.astype(F32) + jnp.einsum(
        "ed,fd->ef", dz_three, w_first, preferred_element_type=F32
    )
    dz_two = (dmixed * silu_slope(z_two)).astype(BF16)
    dagg_t = jnp.einsum("kd,ed->ke", w_up, dz_two, preferred_element_type=F32).astype(BF16)
    partial, basis_local = backward_triplets(
        groups, edges, src, tgt, angle_basis, w_basis, down_in, dagg_t
    )
    ddown_t = collect_down(groups, partial.reshape(groups, width, edges))
    second_local = jnp.einsum("ed,ef->df", inner, dz_four, preferred_element_type=F32)
    first_local = jnp.einsum("ed,ef->df", mixed, dz_three, preferred_element_type=F32)
    up_local = jnp.einsum("ke,ed->kd", agg_t, dz_two, preferred_element_type=F32)
    down_local = jnp.einsum("ed,ke->dk", hidden, ddown_t, preferred_element_type=F32)
    dz_one = (
        jnp.einsum("ke,dk->ed", ddown_t, w_down, preferred_element_type=F32) * silu_slope(z_one)
    ).astype(BF16)
    pair_local = jnp.einsum("ed,ef->df", edge_feats, dz_one, preferred_element_type=F32)
    edge_grad = jnp.einsum("ef,df->ed", dz_one, w_pair, preferred_element_type=F32).astype(BF16)

    def large(item):
        rows, cols = item.shape
        return item.astype(BF16).reshape(n, groups, rows // (n * groups), cols)

    def small(item, kind):
        return item.astype(kind).reshape(n, item.shape[0] // n, item.shape[1])

    second_sum, first_sum, pair_sum, up_sum, down_sum, basis_sum = total_grads(
        n,
        groups,
        (
            large(second_local),
            large(first_local),
            large(pair_local),
            small(up_local, BF16),
            small(down_local, BF16),
            small(basis_local, F32),
        ),
        (True, True, True, False, False, False),
    )
    return (
        edge_grad,
        pair_sum.reshape(-1, pair_sum.shape[2]),
        down_sum,
        basis_sum,
        up_sum,
        first_sum.reshape(-1, first_sum.shape[2]),
        second_sum.reshape(-1, second_sum.shape[2]),
    )


def solution(mesh):
    return jax.shard_map(
        on_device,
        mesh=mesh,
        in_specs=(
            P(("dp", "graph"), None),
            P(("dp", "graph"), None),
            P(None, ("dp", "graph")),
            P(("dp", "graph")),
            P(("dp", "graph")),
            P("dp", None),
            P("dp", None),
            P("dp", None),
            P("dp", None),
            P("dp", None),
            P("dp", None),
        ),
        out_specs=(
            P(("dp", "graph"), None),
            P("dp", None),
            P("dp", None),
            P("dp", None),
            P("dp", None),
            P("dp", None),
            P("dp", None),
        ),
        check_vma=False,
    )
```

```python
import functools
import math

import jax
import jax.numpy as jnp
from jax import lax
from jax.experimental import pallas as pl
from jax.experimental.pallas import tpu as pltpu
from jax.sharding import PartitionSpec as P

MESH = pl.DeviceIdType.MESH
F32 = jnp.float32
BF16 = jnp.bfloat16
VM = pl.BlockSpec(memory_space=pltpu.VMEM)
SUB = 256
TILE = 1024


def remote(src, dst, send, recv, target):
    return pltpu.make_async_remote_copy(
        src_ref=src,
        dst_ref=dst,
        send_sem=send,
        recv_sem=recv,
        device_id=target,
        device_id_type=MESH,
    )


def silu_slope(value):
    sig = jax.nn.sigmoid(value)
    return sig * (1.0 + value * (1.0 - sig))


def greet(targets, waits):
    barrier = pltpu.get_barrier_semaphore()
    for target in targets:
        pl.semaphore_signal(barrier, inc=1, device_id=target, device_id_type=MESH)
    pl.semaphore_wait(barrier, waits)


def graph_peers(groups):
    me = lax.axis_index("graph")
    return [{"graph": (me + k) % groups} for k in range(1, groups)]


def chip_peers(n):
    half = n // 2
    dp = lax.axis_index("dp")
    return [{"dp": (dp // 2 + k) % half * 2 + dp % 2} for k in range(1, half)]


def core_peer():
    dp = lax.axis_index("dp")
    return [{"dp": dp + 1 - 2 * (dp % 2)}]


def gather_steps(n, ins, outs, send, recv):
    count = len(ins)
    half = n // 2
    dp = lax.axis_index("dp")
    pos = dp // 2
    core = dp % 2
    partner = dp + 1 - 2 * core
    has_up = pos < half - 1
    has_down = pos > 0

    def copy(w, src, shard, way, target):
        return remote(
            src, outs[w].at[shard], send.at[shard, way, w], recv.at[shard, w], {"dp": target}
        )

    for w in range(count):

        @pl.when(has_up)
        def _():
            copy(w, ins[w], dp, 0, dp + 2).start()

        @pl.when(has_down)
        def _():
            copy(w, ins[w], dp, 1, dp - 2).start()

        copy(w, ins[w], dp, 2, partner).start()
    for w in range(count):
        outs[w][dp] = ins[w][...]
    yield
    for k in range(1, half):
        for w in range(count):

            @pl.when(pos >= k)
            def _():
                shard = dp - 2 * k
                block = outs[w].at[shard]
                copy(w, block, shard, 2, partner).wait_recv()

                @pl.when(has_up)
                def _():
                    copy(w, block, shard, 0, dp + 2).start()

                copy(w, block, shard, 2, partner).start()

            @pl.when(pos + k < half)
            def _():
                shard = dp + 2 * k
                block = outs[w].at[shard]
                copy(w, block, shard, 2, partner).wait_recv()

                @pl.when(has_down)
                def _():
                    copy(w, block, shard, 1, dp - 2).start()

                copy(w, block, shard, 2, partner).start()

        yield
    for w in range(count):
        for q in range(half):
            shard = 2 * q + 1 - core
            copy(w, outs[w].at[shard], shard, 2, partner).wait_recv()
            mine = 2 * q + core
            copy(w, outs[w].at[mine], mine, 2, partner).wait_send()

            @pl.when(jnp.logical_and(pos >= q, has_up))
            def _():
                copy(w, outs[w].at[mine], mine, 0, dp + 2).wait_send()

            @pl.when(jnp.logical_and(pos <= q, has_down))
            def _():
                copy(w, outs[w].at[mine], mine, 1, dp - 2).wait_send()


def gather_kernel(n, count, *refs):
    greet(chip_peers(n) + core_peer(), n // 2)
    for _ in gather_steps(n, refs[:count], refs[count : 2 * count], *refs[2 * count :]):
        pass


def gather_sems(n, count):
    return [pltpu.SemaphoreType.DMA((n, 3, count)), pltpu.SemaphoreType.DMA((n, count))]


def gathered(n, weights):
    return [jax.ShapeDtypeStruct((n,) + w.shape, w.dtype) for w in weights]


def gather_weights(n, weights):
    count = len(weights)
    return pl.pallas_call(
        functools.partial(gather_kernel, n, count),
        out_shape=gathered(n, weights),
        in_specs=[VM] * count,
        out_specs=[VM] * count,
        scratch_shapes=gather_sems(n, count),
        compiler_params=pltpu.CompilerParams(collective_id=0, has_side_effects=True),
        name="gather_weights",
    )(*weights)


def total_steps(n, groups, kinds, ins, outs, refs):
    count = len(kinds)
    scratch = []
    place_at = 0
    for large in kinds:
        size = 6 if large else 4
        scratch.append(refs[place_at : place_at + size])
        place_at += size
    a_send, a_recv, b_send, b_recv, c_send, c_recv, d_send, d_recv = refs[place_at:]
    half = n // 2
    dp = lax.axis_index("dp")
    me = lax.axis_index("graph")
    pos = dp // 2
    core = dp % 2
    partner = dp + 1 - 2 * core
    sent = []

    def send_all(copies):
        for cp in copies:
            cp.start()
        sent.extend(copies)
        return copies

    first = []
    for w in range(count):
        first.append(
            send_all(
                [
                    remote(
                        ins[w].at[2 * q + 1 - core],
                        scratch[w][0].at[q],
                        a_send.at[w, q],
                        a_recv.at[w, q],
                        {"dp": partner},
                    )
                    for q in range(half)
                ]
            )
        )
    yield
    second = []
    for w, large in enumerate(kinds):
        got, summed = scratch[w][0], scratch[w][1]
        for q in range(half):
            first[w][q].wait_recv()
            value = ins[w][2 * q + core].astype(F32) + got[q].astype(F32)
            if large:
                summed[:, q] = value.astype(summed.dtype)
            else:
                summed[q] = value.astype(summed.dtype)
        copies = []
        if large:
            copies = [
                remote(
                    summed.at[(me + k) % groups],
                    scratch[w][4].at[k],
                    b_send.at[w, k],
                    b_recv.at[w, k],
                    {"graph": (me + k) % groups},
                )
                for k in range(1, groups)
            ]
        second.append(send_all(copies))
    yield
    third = []
    for w, large in enumerate(kinds):
        part = scratch[w][1]
        if large:
            for cp in second[w]:
                cp.wait_recv()
            value = scratch[w][1][me].astype(F32)
            for k in range(1, groups):
                value = value + scratch[w][4][k].astype(F32)
            part = scratch[w][5]
            part[...] = value.astype(part.dtype)
        third.append(
            send_all(
                [
                    remote(
                        part.at[(pos + k) % half],
                        scratch[w][2].at[k],
                        c_send.at[w, k],
                        c_recv.at[w, k],
                        {"dp": (pos + k) % half * 2 + core},
                    )
                    for k in range(1, half)
                ]
            )
        )
    yield
    fourth = []
    for w, large in enumerate(kinds):
        part = scratch[w][5] if large else scratch[w][1]
        for cp in third[w]:
            cp.wait_recv()
        value = part[pos].astype(F32)
        for k in range(1, half):
            value = value + scratch[w][2][k].astype(F32)
        done = scratch[w][3]
        done[...] = value.astype(done.dtype)
        fourth.append(
            send_all(
                [
                    remote(
                        done,
                        outs[w].at[me],
                        d_send.at[w, k],
                        d_recv.at[w, k],
                        {"graph": (me + k) % groups},
                    )
                    for k in range(1, groups)
                ]
            )
        )
        outs[w][me] = value.astype(done.dtype)
    yield
    for copies in fourth:
        for cp in copies:
            cp.wait_recv()
    for cp in sent:
        cp.wait_send()


def total_parts(n, groups, grads, kinds):
    half = n // 2
    shapes, scratch = [], []
    for item, large in zip(grads, kinds):
        tail = item.shape[2:] if large else item.shape[1:]
        kind = item.dtype
        shapes.append(jax.ShapeDtypeStruct((groups,) + tail, kind))
        scratch.append(pltpu.VMEM((half,) + item.shape[1:], kind))
        scratch.append(
            pltpu.VMEM(((groups, half) + tail) if large else ((half,) + tail), kind)
        )
        scratch.append(pltpu.VMEM((half,) + tail, kind))
        scratch.append(pltpu.VMEM(tail, kind))
        if large:
            scratch.append(pltpu.VMEM((groups, half) + tail, kind))
            scratch.append(pltpu.VMEM((half,) + tail, kind))
    for length in (half, groups, half, groups):
        scratch += [pltpu.SemaphoreType.DMA((len(grads), length))] * 2
    return shapes, scratch


def greet_all(n, groups):
    greet(core_peer() + graph_peers(groups) + chip_peers(n), groups + n // 2 - 1)


def total_kernel(n, groups, kinds, *refs):
    count = len(kinds)
    greet_all(n, groups)
    for _ in total_steps(
        n, groups, kinds, refs[:count], refs[count : 2 * count], refs[2 * count :]
    ):
        pass


def total_grads(n, groups, grads, kinds):
    count = len(grads)
    shapes, scratch = total_parts(n, groups, grads, kinds)
    return pl.pallas_call(
        functools.partial(total_kernel, n, groups, kinds),
        out_shape=shapes,
        in_specs=[VM] * count,
        out_specs=[VM] * count,
        scratch_shapes=scratch,
        compiler_params=pltpu.CompilerParams(collective_id=3, has_side_effects=True),
        name="total_grads",
    )(*grads)


def write_kernel(kinds, *refs):
    for large, landed, out in zip(kinds, refs[: len(kinds)], refs[len(kinds) :]):
        groups, rows = landed.shape[0], landed.shape[1]
        if large:
            for g in range(groups):
                out[g * rows : (g + 1) * rows, :] = landed[g].astype(F32)
        else:
            value = landed[0].astype(F32)
            for g in range(1, groups):
                value = value + landed[g].astype(F32)
            out[...] = value


def write_grads(landed, kinds):
    return pl.pallas_call(
        functools.partial(write_kernel, kinds),
        out_shape=[
            jax.ShapeDtypeStruct(
                (item.shape[1] * (item.shape[0] if large else 1), item.shape[2]), F32
            )
            for item, large in zip(landed, kinds)
        ],
        in_specs=[VM] * len(kinds),
        out_specs=[VM] * len(kinds),
        name="write_grads",
    )(*landed)


def one_hot(size, row):
    spots = lax.broadcasted_iota(jnp.int32, (size, row.shape[1]), 0)
    return jnp.where(spots == row, 1.0, 0.0).astype(BF16)


def pick(stack, owner, groups, width):
    value = jnp.where(owner == 0, stack[:width], 0.0)
    for g in range(1, groups):
        value = value + jnp.where(owner == g, stack[g * width : (g + 1) * width], 0.0)
    return value


def place(value, owner, groups):
    return jnp.concatenate(
        [jnp.where(owner == g, value, 0.0).astype(BF16) for g in range(groups)], axis=0
    )


def dot(a, b, dims):
    return lax.dot_general(a, b, (dims, ((), ())), preferred_element_type=F32)


NN = ((1,), (0,))
NT = ((1,), (1,))
TN = ((0,), (0,))


def forward_kernel(
    n,
    groups,
    src_ref,
    tgt_ref,
    basis_ref,
    wb_ref,
    down_ref,
    up_ref,
    first_ref,
    second_ref,
    agg_ref,
    din_ref,
    up_out,
    first_out,
    second_out,
    acc,
    table,
    send,
    recv,
    w_send,
    w_recv,
):
    width, edges = down_ref.shape
    subs = edges // SUB
    trips = src_ref.shape[1]
    tile = min(TILE, trips)
    me = lax.axis_index("graph")
    greet(
        graph_peers(groups) + chip_peers(n) + core_peer(), groups - 1 + n // 2
    )
    copies = []
    for k in range(1, groups):
        cp = remote(
            down_ref, table.at[me], send.at[k], recv.at[k], {"graph": (me + k) % groups}
        )
        cp.start()
        copies.append(cp)
    steps = gather_steps(
        n,
        (up_ref, first_ref, second_ref),
        (up_out, first_out, second_out),
        w_send,
        w_recv,
    )
    table[me] = down_ref[...]
    acc[...] = jnp.zeros_like(acc)

    def work(i, carry):
        spot = pl.ds(pl.multiple_of(i * tile, tile), tile)
        src = src_ref[:, spot]
        tgt = tgt_ref[:, spot]
        basis = basis_ref[:, spot]
        owner = src // edges
        stack = dot(
            table[...].reshape(groups * width, edges), one_hot(edges, src - owner * edges), NN
        )
        down_in = pick(stack, owner, groups, width)
        din_ref[:, spot] = down_in.astype(BF16)
        coeff = dot(wb_ref[...], basis, TN)
        high = tgt // SUB
        acc[...] += dot(
            place(down_in * coeff, high, subs), one_hot(SUB, tgt - high * SUB), NT
        )
        return carry

    next(steps)
    for cp in copies:
        cp.wait()
    tiles = trips // tile
    count = n // 2 - 1
    for i in range(count):
        lax.fori_loop(tiles * i // (count + 1), tiles * (i + 1) // (count + 1), work, 0)
        next(steps)
    lax.fori_loop(tiles * count // (count + 1), tiles, work, 0)
    for h in range(subs):
        agg_ref[:, h * SUB : (h + 1) * SUB] = acc[h * width : (h + 1) * width, :].astype(BF16)
    for _ in steps:
        pass


def forward_triplets(n, groups, src, tgt, basis, w_basis, down, weights):
    trips = src.shape[1]
    width, edges = down.shape
    return pl.pallas_call(
        functools.partial(forward_kernel, n, groups),
        out_shape=[
            jax.ShapeDtypeStruct((width, edges), BF16),
            jax.ShapeDtypeStruct((width, trips), BF16),
        ]
        + gathered(n, weights),
        in_specs=[VM] * 8,
        out_specs=[VM] * 5,
        scratch_shapes=[
            pltpu.VMEM((edges // SUB * width, SUB), F32),
            pltpu.VMEM((groups, width, edges), BF16),
        ]
        + [pltpu.SemaphoreType.DMA((groups,))] * 2
        + gather_sems(n, len(weights)),
        compiler_params=pltpu.CompilerParams(collective_id=1, has_side_effects=True),
        name="forward_triplets",
    )(src, tgt, basis, w_basis, down, *weights)


def backward_kernel(n, groups, kinds, *refs):
    src_ref, tgt_ref, basis_ref, wb_ref, din_ref, dagg_ref = refs[:6]
    count = len(kinds)
    ins = refs[6 : 6 + count]
    ddown_ref, bg_ref = refs[6 + count : 8 + count]
    outs = refs[8 + count : 8 + 2 * count]
    acc, stack_ref, part, landed, send, recv = refs[8 + 2 * count : 14 + 2 * count]
    rest = refs[14 + 2 * count :]
    width, edges = dagg_ref.shape
    subs = edges // SUB
    trips = src_ref.shape[1]
    tile = min(TILE, trips)
    me = lax.axis_index("graph")
    greet_all(n, groups)
    steps = total_steps(n, groups, kinds, ins, outs, rest)
    acc[...] = jnp.zeros_like(acc)
    bg_ref[...] = jnp.zeros_like(bg_ref)
    for h in range(subs):
        stack_ref[h * width : (h + 1) * width, :] = dagg_ref[:, h * SUB : (h + 1) * SUB]

    def work(i, carry):
        spot = pl.ds(pl.multiple_of(i * tile, tile), tile)
        src = src_ref[:, spot]
        tgt = tgt_ref[:, spot]
        basis = basis_ref[:, spot]
        owner = src // edges
        high = tgt // SUB
        dagg_out = pick(
            dot(stack_ref[...], one_hot(SUB, tgt - high * SUB), NN), high, subs, width
        )
        dcoeff = (dagg_out * din_ref[:, spot].astype(F32)).astype(BF16)
        bg_ref[...] += dot(basis, dcoeff, NT)
        coeff = dot(wb_ref[...], basis, TN)
        acc[...] += dot(
            place(dagg_out * coeff, owner, groups), one_hot(edges, src - owner * edges), NT
        )
        return carry

    tiles = trips // tile
    for i in range(4):
        next(steps)
        lax.fori_loop(tiles * i // 4, tiles * (i + 1) // 4, work, 0)
    for g in range(groups):
        part[g] = acc[g * width : (g + 1) * width, :].astype(BF16)
    copies = []
    for k in range(1, groups):
        peer = (me + k) % groups
        cp = remote(part.at[peer], landed.at[k], send.at[k], recv.at[k], {"graph": peer})
        cp.start()
        copies.append(cp)
    for _ in steps:
        pass
    for cp in copies:
        cp.wait()
    total = part[me].astype(F32)
    for k in range(1, groups):
        total = total + landed[k].astype(F32)
    ddown_ref[...] = total.astype(BF16)


def backward_triplets(n, groups, src, tgt, basis, w_basis, down_in, dagg, grads, kinds):
    width, edges = dagg.shape
    shapes, scratch = total_parts(n, groups, grads, kinds)
    return pl.pallas_call(
        functools.partial(backward_kernel, n, groups, kinds),
        out_shape=[
            jax.ShapeDtypeStruct((width, edges), BF16),
            jax.ShapeDtypeStruct(w_basis.shape, F32),
        ]
        + shapes,
        in_specs=[VM] * (6 + len(grads)),
        out_specs=[VM] * (2 + len(grads)),
        scratch_shapes=[
            pltpu.VMEM((groups * width, edges), F32),
            pltpu.VMEM((edges // SUB * width, SUB), BF16),
            pltpu.VMEM((groups, width, edges), BF16),
            pltpu.VMEM((groups, width, edges), BF16),
        ]
        + [pltpu.SemaphoreType.DMA((groups,))] * 2
        + scratch,
        compiler_params=pltpu.CompilerParams(collective_id=2, has_side_effects=True),
        name="backward_triplets",
    )(src, tgt, basis, w_basis, down_in, dagg, *grads)


def on_device(
    edge_feats,
    cotangent,
    angle_basis,
    source_edge,
    target_edge,
    pair_weight,
    down_weight,
    basis_weight,
    up_weight,
    res_first,
    res_second,
):
    scale = math.sqrt(0.5)
    n = lax.axis_size("dp")
    groups = lax.axis_size("graph")
    def whole(item):
        return item.reshape(-1, item.shape[2])

    def large(item):
        rows, cols = item.shape
        return item.astype(BF16).reshape(n, groups, rows // (n * groups), cols)

    def small(item, kind):
        return item.astype(kind).reshape(n, item.shape[0] // n, item.shape[1])

    w_pair, w_down, w_basis = map(
        whole, gather_weights(n, (pair_weight, down_weight, basis_weight))
    )
    src = source_edge.reshape(1, -1)
    tgt = target_edge.reshape(1, -1)
    z_one = jnp.dot(edge_feats, w_pair, preferred_element_type=F32)
    hidden = jax.nn.silu(z_one).astype(BF16)
    down_t = jnp.einsum("ed,dk->ke", hidden, w_down, preferred_element_type=F32).astype(BF16)
    agg_t, down_in, w_up, w_first, w_second = forward_triplets(
        n,
        groups,
        src,
        tgt,
        angle_basis,
        w_basis,
        down_t,
        (up_weight, res_first, res_second),
    )
    w_up, w_first, w_second = whole(w_up), whole(w_first), whole(w_second)
    z_two = jnp.einsum("ke,kd->ed", agg_t, w_up, preferred_element_type=F32)
    mixed = jax.nn.silu(z_two).astype(BF16)
    z_three = jnp.dot(mixed, w_first, preferred_element_type=F32)
    inner = jax.nn.silu(z_three).astype(BF16)
    z_four = jnp.dot(inner, w_second, preferred_element_type=F32)
    dz_four = (scale * cotangent.astype(F32) * silu_slope(z_four)).astype(BF16)
    dz_three = (
        jnp.einsum("ed,fd->ef", dz_four, w_second, preferred_element_type=F32) * silu_slope(z_three)
    ).astype(BF16)
    dmixed = scale * cotangent.astype(F32) + jnp.einsum(
        "ed,fd->ef", dz_three, w_first, preferred_element_type=F32
    )
    dz_two = (dmixed * silu_slope(z_two)).astype(BF16)
    dagg_t = jnp.einsum("kd,ed->ke", w_up, dz_two, preferred_element_type=F32).astype(BF16)
    second_local = jnp.einsum("ed,ef->df", inner, dz_four, preferred_element_type=F32)
    first_local = jnp.einsum("ed,ef->df", mixed, dz_three, preferred_element_type=F32)
    up_local = jnp.einsum("ke,ed->kd", agg_t, dz_two, preferred_element_type=F32)
    ddown_t, basis_local, second_land, first_land, up_land = backward_triplets(
        n,
        groups,
        src,
        tgt,
        angle_basis,
        w_basis,
        down_in,
        dagg_t,
        (large(second_local), large(first_local), small(up_local, BF16)),
        (True, True, False),
    )
    down_local = jnp.einsum("ed,ke->dk", hidden, ddown_t, preferred_element_type=F32)
    dz_one = (
        jnp.einsum("ke,dk->ed", ddown_t, w_down, preferred_element_type=F32) * silu_slope(z_one)
    ).astype(BF16)
    pair_local = jnp.einsum("ed,ef->df", edge_feats, dz_one, preferred_element_type=F32)
    edge_grad = jnp.einsum("ef,df->ed", dz_one, w_pair, preferred_element_type=F32).astype(BF16)

    pair_land, down_land, basis_land = total_grads(
        n,
        groups,
        (large(pair_local), small(down_local, BF16), small(basis_local, F32)),
        (True, False, False),
    )
    return (
        edge_grad,
        *write_grads(
            (pair_land, down_land, basis_land, up_land, first_land, second_land),
            (True, False, False, False, True, True),
        ),
    )


def solution(mesh):
    return jax.shard_map(
        on_device,
        mesh=mesh,
        in_specs=(
            P(("dp", "graph"), None),
            P(("dp", "graph"), None),
            P(None, ("dp", "graph")),
            P(("dp", "graph")),
            P(("dp", "graph")),
            P("dp", None),
            P("dp", None),
            P("dp", None),
            P("dp", None),
            P("dp", None),
            P("dp", None),
        ),
        out_specs=(
            P(("dp", "graph"), None),
            P("dp", None),
            P("dp", None),
            P("dp", None),
            P("dp", None),
            P("dp", None),
            P("dp", None),
        ),
        check_vma=False,
    )
```

```python
import functools
import math

import jax
import jax.numpy as jnp
from jax import lax
from jax.experimental import pallas as pl
from jax.experimental.pallas import tpu as pltpu
from jax.sharding import PartitionSpec as P

MESH = pl.DeviceIdType.MESH
F32 = jnp.float32
BF16 = jnp.bfloat16
VM = pl.BlockSpec(memory_space=pltpu.VMEM)
SUB = 256
TILE = 1024


def remote(src, dst, send, recv, target):
    return pltpu.make_async_remote_copy(
        src_ref=src,
        dst_ref=dst,
        send_sem=send,
        recv_sem=recv,
        device_id=target,
        device_id_type=MESH,
    )


def silu_slope(value):
    sig = jax.nn.sigmoid(value)
    return sig * (1.0 + value * (1.0 - sig))


def greet(targets, waits):
    barrier = pltpu.get_barrier_semaphore()
    for target in targets:
        pl.semaphore_signal(barrier, inc=1, device_id=target, device_id_type=MESH)
    pl.semaphore_wait(barrier, waits)


def graph_peers(groups):
    me = lax.axis_index("graph")
    return [{"graph": (me + k) % groups} for k in range(1, groups)]


def chip_peers(n):
    half = n // 2
    dp = lax.axis_index("dp")
    return [{"dp": (dp // 2 + k) % half * 2 + dp % 2} for k in range(1, half)]


def core_peer():
    dp = lax.axis_index("dp")
    return [{"dp": dp + 1 - 2 * (dp % 2)}]


def gather_steps(n, ins, outs, send, recv):
    count = len(ins)
    half = n // 2
    dp = lax.axis_index("dp")
    pos = dp // 2
    core = dp % 2
    partner = dp + 1 - 2 * core
    has_up = pos < half - 1
    has_down = pos > 0

    def copy(w, src, shard, way, target):
        return remote(
            src, outs[w].at[shard], send.at[shard, way, w], recv.at[shard, w], {"dp": target}
        )

    for w in range(count):

        @pl.when(has_up)
        def _():
            copy(w, ins[w], dp, 0, dp + 2).start()

        @pl.when(has_down)
        def _():
            copy(w, ins[w], dp, 1, dp - 2).start()

        copy(w, ins[w], dp, 2, partner).start()
    for w in range(count):
        outs[w][dp] = ins[w][...]
    yield
    for k in range(1, half):
        for w in range(count):

            @pl.when(pos >= k)
            def _():
                shard = dp - 2 * k
                block = outs[w].at[shard]
                copy(w, block, shard, 2, partner).wait_recv()

                @pl.when(has_up)
                def _():
                    copy(w, block, shard, 0, dp + 2).start()

                copy(w, block, shard, 2, partner).start()

            @pl.when(pos + k < half)
            def _():
                shard = dp + 2 * k
                block = outs[w].at[shard]
                copy(w, block, shard, 2, partner).wait_recv()

                @pl.when(has_down)
                def _():
                    copy(w, block, shard, 1, dp - 2).start()

                copy(w, block, shard, 2, partner).start()

        yield
    for w in range(count):
        for q in range(half):
            shard = 2 * q + 1 - core
            copy(w, outs[w].at[shard], shard, 2, partner).wait_recv()
            mine = 2 * q + core
            copy(w, outs[w].at[mine], mine, 2, partner).wait_send()

            @pl.when(jnp.logical_and(pos >= q, has_up))
            def _():
                copy(w, outs[w].at[mine], mine, 0, dp + 2).wait_send()

            @pl.when(jnp.logical_and(pos <= q, has_down))
            def _():
                copy(w, outs[w].at[mine], mine, 1, dp - 2).wait_send()


def gather_kernel(n, count, *refs):
    greet(chip_peers(n) + core_peer(), n // 2)
    for _ in gather_steps(n, refs[:count], refs[count : 2 * count], *refs[2 * count :]):
        pass


def gather_sems(n, count):
    return [pltpu.SemaphoreType.DMA((n, 3, count)), pltpu.SemaphoreType.DMA((n, count))]


def gathered(n, weights):
    return [jax.ShapeDtypeStruct((n,) + w.shape, w.dtype) for w in weights]


def gather_weights(n, weights):
    count = len(weights)
    return pl.pallas_call(
        functools.partial(gather_kernel, n, count),
        out_shape=gathered(n, weights),
        in_specs=[VM] * count,
        out_specs=[VM] * count,
        scratch_shapes=gather_sems(n, count),
        compiler_params=pltpu.CompilerParams(collective_id=0, has_side_effects=True),
        name="gather_weights",
    )(*weights)


def total_steps(n, groups, kinds, ins, outs, refs):
    count = len(kinds)
    scratch = []
    place_at = 0
    for large in kinds:
        size = 6 if large else 4
        scratch.append(refs[place_at : place_at + size])
        place_at += size
    a_send, a_recv, b_send, b_recv, c_send, c_recv, d_send, d_recv = refs[place_at:]
    half = n // 2
    dp = lax.axis_index("dp")
    me = lax.axis_index("graph")
    pos = dp // 2
    core = dp % 2
    partner = dp + 1 - 2 * core
    sent = []

    def send_all(copies):
        for cp in copies:
            cp.start()
        sent.extend(copies)
        return copies

    first = []
    for w in range(count):
        first.append(
            send_all(
                [
                    remote(
                        ins[w].at[2 * q + 1 - core],
                        scratch[w][0].at[q],
                        a_send.at[w, q],
                        a_recv.at[w, q],
                        {"dp": partner},
                    )
                    for q in range(half)
                ]
            )
        )
    yield
    second = []
    for w, large in enumerate(kinds):
        got, summed = scratch[w][0], scratch[w][1]
        for q in range(half):
            first[w][q].wait_recv()
            value = ins[w][2 * q + core].astype(F32) + got[q].astype(F32)
            if large:
                summed[:, q] = value.astype(summed.dtype)
            else:
                summed[q] = value.astype(summed.dtype)
        copies = []
        if large:
            copies = [
                remote(
                    summed.at[(me + k) % groups],
                    scratch[w][4].at[k],
                    b_send.at[w, k],
                    b_recv.at[w, k],
                    {"graph": (me + k) % groups},
                )
                for k in range(1, groups)
            ]
        second.append(send_all(copies))
    yield
    third = []
    for w, large in enumerate(kinds):
        part = scratch[w][1]
        if large:
            for cp in second[w]:
                cp.wait_recv()
            value = scratch[w][1][me].astype(F32)
            for k in range(1, groups):
                value = value + scratch[w][4][k].astype(F32)
            part = scratch[w][5]
            part[...] = value.astype(part.dtype)
        third.append(
            send_all(
                [
                    remote(
                        part.at[(pos + k) % half],
                        scratch[w][2].at[k],
                        c_send.at[w, k],
                        c_recv.at[w, k],
                        {"dp": (pos + k) % half * 2 + core},
                    )
                    for k in range(1, half)
                ]
            )
        )
    yield
    fourth = []
    for w, large in enumerate(kinds):
        part = scratch[w][5] if large else scratch[w][1]
        for cp in third[w]:
            cp.wait_recv()
        value = part[pos].astype(F32)
        for k in range(1, half):
            value = value + scratch[w][2][k].astype(F32)
        done = scratch[w][3]
        done[...] = value.astype(done.dtype)
        fourth.append(
            send_all(
                [
                    remote(
                        done,
                        outs[w].at[me],
                        d_send.at[w, k],
                        d_recv.at[w, k],
                        {"graph": (me + k) % groups},
                    )
                    for k in range(1, groups)
                ]
            )
        )
        outs[w][me] = value.astype(done.dtype)
    yield
    for copies in fourth:
        for cp in copies:
            cp.wait_recv()
    for cp in sent:
        cp.wait_send()


def total_parts(n, groups, grads, kinds):
    half = n // 2
    shapes, scratch = [], []
    for item, large in zip(grads, kinds):
        tail = item.shape[2:] if large else item.shape[1:]
        kind = item.dtype
        shapes.append(jax.ShapeDtypeStruct((groups,) + tail, kind))
        scratch.append(pltpu.VMEM((half,) + item.shape[1:], kind))
        scratch.append(
            pltpu.VMEM(((groups, half) + tail) if large else ((half,) + tail), kind)
        )
        scratch.append(pltpu.VMEM((half,) + tail, kind))
        scratch.append(pltpu.VMEM(tail, kind))
        if large:
            scratch.append(pltpu.VMEM((groups, half) + tail, kind))
            scratch.append(pltpu.VMEM((half,) + tail, kind))
    for length in (half, groups, half, groups):
        scratch += [pltpu.SemaphoreType.DMA((len(grads), length))] * 2
    return shapes, scratch


def greet_all(n, groups):
    greet(core_peer() + graph_peers(groups) + chip_peers(n), groups + n // 2 - 1)


def total_kernel(n, groups, kinds, *refs):
    count = len(kinds)
    greet_all(n, groups)
    for _ in total_steps(
        n, groups, kinds, refs[:count], refs[count : 2 * count], refs[2 * count :]
    ):
        pass


def total_grads(n, groups, grads, kinds):
    count = len(grads)
    shapes, scratch = total_parts(n, groups, grads, kinds)
    return pl.pallas_call(
        functools.partial(total_kernel, n, groups, kinds),
        out_shape=shapes,
        in_specs=[VM] * count,
        out_specs=[VM] * count,
        scratch_shapes=scratch,
        compiler_params=pltpu.CompilerParams(collective_id=3, has_side_effects=True),
        name="total_grads",
    )(*grads)


def write_kernel(kinds, *refs):
    for large, landed, out in zip(kinds, refs[: len(kinds)], refs[len(kinds) :]):
        groups, rows = landed.shape[0], landed.shape[1]
        if large:
            for g in range(groups):
                out[g * rows : (g + 1) * rows, :] = landed[g].astype(F32)
        else:
            value = landed[0].astype(F32)
            for g in range(1, groups):
                value = value + landed[g].astype(F32)
            out[...] = value


def write_grads(landed, kinds):
    return pl.pallas_call(
        functools.partial(write_kernel, kinds),
        out_shape=[
            jax.ShapeDtypeStruct(
                (item.shape[1] * (item.shape[0] if large else 1), item.shape[2]), F32
            )
            for item, large in zip(landed, kinds)
        ],
        in_specs=[VM] * len(kinds),
        out_specs=[VM] * len(kinds),
        name="write_grads",
    )(*landed)


def one_hot(size, row):
    spots = lax.broadcasted_iota(jnp.int32, (size, row.shape[1]), 0)
    return jnp.where(spots == row, 1.0, 0.0).astype(BF16)


def pick(stack, owner, groups, width):
    value = jnp.where(owner == 0, stack[:width], 0.0)
    for g in range(1, groups):
        value = value + jnp.where(owner == g, stack[g * width : (g + 1) * width], 0.0)
    return value


def place(value, owner, groups):
    return jnp.concatenate(
        [jnp.where(owner == g, value, 0.0).astype(BF16) for g in range(groups)], axis=0
    )


def dot(a, b, dims):
    return lax.dot_general(a, b, (dims, ((), ())), preferred_element_type=F32)


NN = ((1,), (0,))
NT = ((1,), (1,))
TN = ((0,), (0,))


def forward_kernel(
    n,
    groups,
    src_ref,
    tgt_ref,
    basis_ref,
    wb_ref,
    down_ref,
    up_ref,
    first_ref,
    second_ref,
    agg_ref,
    din_ref,
    up_out,
    first_out,
    second_out,
    acc,
    table,
    send,
    recv,
    w_send,
    w_recv,
):
    width, edges = down_ref.shape
    subs = edges // SUB
    trips = src_ref.shape[1]
    tile = min(TILE, trips)
    me = lax.axis_index("graph")
    greet(
        graph_peers(groups) + chip_peers(n) + core_peer(), groups - 1 + n // 2
    )
    copies = []
    for k in range(1, groups):
        cp = remote(
            down_ref, table.at[me], send.at[k], recv.at[k], {"graph": (me + k) % groups}
        )
        cp.start()
        copies.append(cp)
    steps = gather_steps(
        n,
        (up_ref, first_ref, second_ref),
        (up_out, first_out, second_out),
        w_send,
        w_recv,
    )
    table[me] = down_ref[...]
    acc[...] = jnp.zeros_like(acc)

    def work(i, carry):
        spot = pl.ds(pl.multiple_of(i * tile, tile), tile)
        src = src_ref[:, spot]
        tgt = tgt_ref[:, spot]
        basis = basis_ref[:, spot]
        owner = src // edges
        stack = dot(
            table[...].reshape(groups * width, edges), one_hot(edges, src - owner * edges), NN
        )
        down_in = pick(stack, owner, groups, width)
        din_ref[:, spot] = down_in.astype(BF16)
        coeff = dot(wb_ref[...], basis, TN)
        high = tgt // SUB
        acc[...] += dot(
            place(down_in * coeff, high, subs), one_hot(SUB, tgt - high * SUB), NT
        )
        return carry

    next(steps)
    next(steps, None)
    for cp in copies:
        cp.wait()
    tiles = trips // tile
    count = max(n // 2 - 2, 1)
    for i in range(count):
        next(steps, None)
        lax.fori_loop(tiles * i // count, tiles * (i + 1) // count, work, 0)
    for h in range(subs):
        agg_ref[:, h * SUB : (h + 1) * SUB] = acc[h * width : (h + 1) * width, :].astype(BF16)
    for _ in steps:
        pass


def forward_triplets(n, groups, src, tgt, basis, w_basis, down, weights):
    trips = src.shape[1]
    width, edges = down.shape
    return pl.pallas_call(
        functools.partial(forward_kernel, n, groups),
        out_shape=[
            jax.ShapeDtypeStruct((width, edges), BF16),
            jax.ShapeDtypeStruct((width, trips), BF16),
        ]
        + gathered(n, weights),
        in_specs=[VM] * 8,
        out_specs=[VM] * 5,
        scratch_shapes=[
            pltpu.VMEM((edges // SUB * width, SUB), F32),
            pltpu.VMEM((groups, width, edges), BF16),
        ]
        + [pltpu.SemaphoreType.DMA((groups,))] * 2
        + gather_sems(n, len(weights)),
        compiler_params=pltpu.CompilerParams(collective_id=1, has_side_effects=True),
        name="forward_triplets",
    )(src, tgt, basis, w_basis, down, *weights)


def backward_kernel(n, groups, kinds, *refs):
    src_ref, tgt_ref, basis_ref, wb_ref, din_ref, dagg_ref = refs[:6]
    count = len(kinds)
    ins = refs[6 : 6 + count]
    ddown_ref, bg_ref = refs[6 + count : 8 + count]
    outs = refs[8 + count : 8 + 2 * count]
    acc, stack_ref, part, landed, send, recv = refs[8 + 2 * count : 14 + 2 * count]
    rest = refs[14 + 2 * count :]
    width, edges = dagg_ref.shape
    subs = edges // SUB
    trips = src_ref.shape[1]
    tile = min(TILE, trips)
    me = lax.axis_index("graph")
    greet_all(n, groups)
    steps = total_steps(n, groups, kinds, ins, outs, rest)
    acc[...] = jnp.zeros_like(acc)
    bg_ref[...] = jnp.zeros_like(bg_ref)
    for h in range(subs):
        stack_ref[h * width : (h + 1) * width, :] = dagg_ref[:, h * SUB : (h + 1) * SUB]

    def work(i, carry):
        spot = pl.ds(pl.multiple_of(i * tile, tile), tile)
        src = src_ref[:, spot]
        tgt = tgt_ref[:, spot]
        basis = basis_ref[:, spot]
        owner = src // edges
        high = tgt // SUB
        dagg_out = pick(
            dot(stack_ref[...], one_hot(SUB, tgt - high * SUB), NN), high, subs, width
        )
        dcoeff = (dagg_out * din_ref[:, spot].astype(F32)).astype(BF16)
        bg_ref[...] += dot(basis, dcoeff, NT)
        coeff = dot(wb_ref[...], basis, TN)
        acc[...] += dot(
            place(dagg_out * coeff, owner, groups), one_hot(edges, src - owner * edges), NT
        )
        return carry

    tiles = trips // tile
    cuts = (0, tiles // 8, tiles * 5 // 8, tiles * 7 // 8, tiles)
    for low, high in zip(cuts[:-1], cuts[1:]):
        next(steps)
        lax.fori_loop(low, high, work, 0)
    for g in range(groups):
        part[g] = acc[g * width : (g + 1) * width, :].astype(BF16)
    copies = []
    for k in range(1, groups):
        peer = (me + k) % groups
        cp = remote(part.at[peer], landed.at[k], send.at[k], recv.at[k], {"graph": peer})
        cp.start()
        copies.append(cp)
    for _ in steps:
        pass
    for cp in copies:
        cp.wait()
    total = part[me].astype(F32)
    for k in range(1, groups):
        total = total + landed[k].astype(F32)
    ddown_ref[...] = total.astype(BF16)


def backward_triplets(n, groups, src, tgt, basis, w_basis, down_in, dagg, grads, kinds):
    width, edges = dagg.shape
    shapes, scratch = total_parts(n, groups, grads, kinds)
    return pl.pallas_call(
        functools.partial(backward_kernel, n, groups, kinds),
        out_shape=[
            jax.ShapeDtypeStruct((width, edges), BF16),
            jax.ShapeDtypeStruct(w_basis.shape, F32),
        ]
        + shapes,
        in_specs=[VM] * (6 + len(grads)),
        out_specs=[VM] * (2 + len(grads)),
        scratch_shapes=[
            pltpu.VMEM((groups * width, edges), F32),
            pltpu.VMEM((edges // SUB * width, SUB), BF16),
            pltpu.VMEM((groups, width, edges), BF16),
            pltpu.VMEM((groups, width, edges), BF16),
        ]
        + [pltpu.SemaphoreType.DMA((groups,))] * 2
        + scratch,
        compiler_params=pltpu.CompilerParams(collective_id=2, has_side_effects=True),
        name="backward_triplets",
    )(src, tgt, basis, w_basis, down_in, dagg, *grads)


def on_device(
    edge_feats,
    cotangent,
    angle_basis,
    source_edge,
    target_edge,
    pair_weight,
    down_weight,
    basis_weight,
    up_weight,
    res_first,
    res_second,
):
    scale = math.sqrt(0.5)
    n = lax.axis_size("dp")
    groups = lax.axis_size("graph")
    def whole(item):
        return item.reshape(-1, item.shape[2])

    def large(item):
        rows, cols = item.shape
        return item.astype(BF16).reshape(n, groups, rows // (n * groups), cols)

    def small(item, kind):
        return item.astype(kind).reshape(n, item.shape[0] // n, item.shape[1])

    w_pair, w_down, w_basis = map(
        whole, gather_weights(n, (pair_weight, down_weight, basis_weight))
    )
    src = source_edge.reshape(1, -1)
    tgt = target_edge.reshape(1, -1)
    z_one = jnp.dot(edge_feats, w_pair, preferred_element_type=F32)
    hidden = jax.nn.silu(z_one).astype(BF16)
    down_t = jnp.einsum("ed,dk->ke", hidden, w_down, preferred_element_type=F32).astype(BF16)
    agg_t, down_in, w_up, w_first, w_second = forward_triplets(
        n,
        groups,
        src,
        tgt,
        angle_basis,
        w_basis,
        down_t,
        (up_weight, res_first, res_second),
    )
    w_up, w_first, w_second = whole(w_up), whole(w_first), whole(w_second)
    z_two = jnp.einsum("ke,kd->ed", agg_t, w_up, preferred_element_type=F32)
    mixed = jax.nn.silu(z_two).astype(BF16)
    z_three = jnp.dot(mixed, w_first, preferred_element_type=F32)
    inner = jax.nn.silu(z_three).astype(BF16)
    z_four = jnp.dot(inner, w_second, preferred_element_type=F32)
    dz_four = (scale * cotangent.astype(F32) * silu_slope(z_four)).astype(BF16)
    dz_three = (
        jnp.einsum("ed,fd->ef", dz_four, w_second, preferred_element_type=F32) * silu_slope(z_three)
    ).astype(BF16)
    dmixed = scale * cotangent.astype(F32) + jnp.einsum(
        "ed,fd->ef", dz_three, w_first, preferred_element_type=F32
    )
    dz_two = (dmixed * silu_slope(z_two)).astype(BF16)
    dagg_t = jnp.einsum("kd,ed->ke", w_up, dz_two, preferred_element_type=F32).astype(BF16)
    second_local = jnp.einsum("ed,ef->df", inner, dz_four, preferred_element_type=F32)
    first_local = jnp.einsum("ed,ef->df", mixed, dz_three, preferred_element_type=F32)
    up_local = jnp.einsum("ke,ed->kd", agg_t, dz_two, preferred_element_type=F32)
    ddown_t, basis_local, second_land, first_land, up_land = backward_triplets(
        n,
        groups,
        src,
        tgt,
        angle_basis,
        w_basis,
        down_in,
        dagg_t,
        (large(second_local), large(first_local), small(up_local, BF16)),
        (True, True, False),
    )
    down_local = jnp.einsum("ed,ke->dk", hidden, ddown_t, preferred_element_type=F32)
    dz_one = (
        jnp.einsum("ke,dk->ed", ddown_t, w_down, preferred_element_type=F32) * silu_slope(z_one)
    ).astype(BF16)
    pair_local = jnp.einsum("ed,ef->df", edge_feats, dz_one, preferred_element_type=F32)
    edge_grad = jnp.einsum("ef,df->ed", dz_one, w_pair, preferred_element_type=F32).astype(BF16)

    pair_land, down_land, basis_land = total_grads(
        n,
        groups,
        (large(pair_local), small(down_local, BF16), small(basis_local, F32)),
        (True, False, False),
    )
    return (
        edge_grad,
        *write_grads(
            (pair_land, down_land, basis_land, up_land, first_land, second_land),
            (True, False, False, False, True, True),
        ),
    )


def solution(mesh):
    return jax.shard_map(
        on_device,
        mesh=mesh,
        in_specs=(
            P(("dp", "graph"), None),
            P(("dp", "graph"), None),
            P(None, ("dp", "graph")),
            P(("dp", "graph")),
            P(("dp", "graph")),
            P("dp", None),
            P("dp", None),
            P("dp", None),
            P("dp", None),
            P("dp", None),
            P("dp", None),
        ),
        out_specs=(
            P(("dp", "graph"), None),
            P("dp", None),
            P("dp", None),
            P("dp", None),
            P("dp", None),
            P("dp", None),
            P("dp", None),
        ),
        check_vma=False,
    )
```
